512 devices in a mesh: pp: 8 (over x, z_lo), ep: 64 (over y, z_hi, core).
Axes of the slice: x: 4, y: 8, z: 8 (z_hi: 4, z_lo: 2; z = z_hi * 2 + z_lo), core: 2. Of those that a mesh axis runs over, the one named last changes fastest.
Arguments:
- fwd_act: bfloat16 [8, 4096, 3584], P('pp', 'ep'), may hold values from -6 to 6
- fwd_route: int32 [8, 4096, 1], P('pp', 'ep'), may hold values from 0 to 7, as said below
- fwd_gate: float32 [8, 4096, 1], P('pp', 'ep'), may hold values from 0.25 to 2
- bwd_act: bfloat16 [8, 4096, 3584], P('pp', 'ep'), may hold values from -6 to 6
- bwd_grad: bfloat16 [8, 4096, 3584], P('pp', 'ep'), may hold values from -6 to 6
- bwd_route: int32 [8, 4096, 1], P('pp', 'ep'), may hold values from 0 to 7, as said below
- bwd_gate: float32 [8, 4096, 1], P('pp', 'ep'), may hold values from 0.25 to 2
- norm_gain: float32 [8, 3584], P('pp'), may hold values from 0.25 to 1.75
- w_gate: bfloat16 [8, 64, 1792, 256], P('pp', 'ep'), may hold values from -0.09375 to 0.09375
- w_up: bfloat16 [8, 64, 1792, 256], P('pp', 'ep'), may hold values from -0.09375 to 0.09375
- w_down: bfloat16 [8, 64, 256, 1792], P('pp', 'ep'), may hold values from -0.1875 to 0.1875
Outputs:
- fwd_next: bfloat16 [8, 4096, 3584], P('pp', 'ep')
- bwd_next: bfloat16 [8, 4096, 3584], P('pp', 'ep')
The draws below stay inside these ranges and needn't reach their ends.
Inputs may be any that keep to these rules, and one draw needn't show every extreme that they name: `fwd_route`: among the 64 rows of one device, no expert is named more than 10 times; at each section one expert is named exactly 10 times in every device's rows. `bwd_route`: as fwd_route, drawn independently.
All inputs are finite; a program needn't handle non-finite values.
Results may differ from the reference program's by a relative error of at most 0.011.
Values may be sent and summed in bfloat16 or wider, within the bound.
A program may use at most 128 MiB of HBM per device.

```python
import math
import jax
import jax.numpy as jnp
from jax import lax

D = 3584
H = 1024
SLICES = 8
TOPK = 1
TA = 64
EXPERTS = 8
HB = 256
CAP = 10
TOK = 4096
N_PP = 8
N_EP = 64


def route_helper(key, salt):
    mixed = jax.random.fold_in(key, salt)
    section_key, device_key = jax.random.split(mixed)
    favoured = jax.random.randint(section_key, (N_PP,), 0, EXPERTS, dtype=jnp.int32)

    def one_device(device_rand, chosen):
        label_key, order_key = jax.random.split(device_rand)
        labels = jnp.arange((EXPERTS - 1) * CAP, dtype=jnp.int32) // CAP
        labels = jax.random.permutation(label_key, labels)[:TA - CAP]
        labels = labels + (labels >= chosen).astype(jnp.int32)
        merged = jnp.concatenate([jnp.full((CAP,), chosen, dtype=jnp.int32), labels])
        return jax.random.permutation(order_key, merged)
    device_keys = jax.random.split(device_key, N_PP * N_EP)
    chosen_all = jnp.repeat(favoured, N_EP)
    routes = jax.vmap(one_device)(device_keys, chosen_all)
    return routes.reshape(N_PP, TOK, TOPK).astype(jnp.int32)


def draw_fwd_route(key, part):
    return route_helper(key, 11)


def draw_bwd_route(key, part):
    return route_helper(key, 23)


def block_scale(key, shape, cuts, low, high):
    loudness, own = 1.0, jax.random.fold_in(key, 6)
    for dim, shards_of in cuts:
        draws = jnp.exp(jax.random.uniform(jax.random.fold_in(own, dim), (shards_of,), jnp.float32, low / len(cuts), high / len(cuts)))
        loudness = loudness * jnp.repeat(draws, shape[dim] // shards_of).reshape([-1 if axis == dim else 1 for axis in range(len(shape))])
    return loudness


def gaussian(rng, dims, width, reach, shards=(), kind=jnp.bfloat16):
    gain = block_scale(rng, dims, shards, -0.22, 0.18) if shards else 1.0
    entries = jax.random.normal(rng, dims, jnp.float32) * width * gain
    return jnp.minimum(jnp.maximum(entries, -reach), reach).astype(kind)


def setup_inputs(seed: int = 0) -> dict:
    arg_keys = jax.random.split(jax.random.key(seed), 12)
    fwd_act = gaussian(arg_keys[0], (N_PP, TOK, D), 1.0, 6.0, ((0, 8), (1, 64)))
    fwd_route = draw_fwd_route(jax.random.fold_in(arg_keys[11], 71), 0)
    fwd_gate = jnp.clip(jnp.exp(math.log(2.0) - 2.0794415 * jax.random.uniform(arg_keys[2], (N_PP, TOK, TOPK), jnp.float32) ** block_scale(arg_keys[2], (N_PP, TOK, TOPK), ((0, 8), (1, 64)), -0.2, 0.2)), 0.25, 2.0)
    bwd_act = gaussian(arg_keys[3], (N_PP, TOK, D), 1.0, 6.0, ((0, 8), (1, 64)))
    bwd_grad = gaussian(arg_keys[4], (N_PP, TOK, D), 1.0, 6.0, ((0, 8), (1, 64)))
    bwd_route = draw_bwd_route(jax.random.fold_in(arg_keys[11], 71), 0)
    bwd_gate = jnp.clip(jnp.exp(math.log(2.0) - 2.0794415 * jax.random.uniform(arg_keys[6], (N_PP, TOK, TOPK), jnp.float32) ** block_scale(arg_keys[6], (N_PP, TOK, TOPK), ((0, 8), (1, 64)), -0.2, 0.2)), 0.25, 2.0)
    norm_gain = jnp.clip(1.0 + 0.15 * jax.random.normal(arg_keys[7], (N_PP, D), jnp.float32), 0.25, 1.75)
    w_gate = gaussian(arg_keys[8], (N_PP, N_EP, D // 2, HB), D ** -0.5, 0.09375, ((0, 8), (1, 64)))
    w_up = gaussian(arg_keys[9], (N_PP, N_EP, D // 2, HB), D ** -0.5, 0.09375, ((0, 8), (1, 64)))
    w_down = gaussian(arg_keys[10], (N_PP, N_EP, HB, D // 2), H ** -0.5, 0.1875, ((0, 8), (1, 64)))
    return {"fwd_act": fwd_act, "fwd_route": fwd_route, "fwd_gate": fwd_gate, "bwd_act": bwd_act, "bwd_grad": bwd_grad, "bwd_route": bwd_route, "bwd_gate": bwd_gate, "norm_gain": norm_gain, "w_gate": w_gate, "w_up": w_up, "w_down": w_down}


def normalize(values, norm_scale):
    widened = values.astype(jnp.float32)
    inverse = lax.rsqrt(lax.optimization_barrier(jnp.mean(widened * widened, axis=-1, keepdims=True)) + 1e-06)
    return ((widened * inverse * norm_scale).astype(jnp.bfloat16), inverse)

def build_slots(route_ids):
    by_source = route_ids.reshape(N_EP, TA)
    onehot = (by_source[:, :, None] == jnp.arange(EXPERTS, dtype=jnp.int32)[None, None, :]).astype(jnp.int32)
    running = jnp.cumsum(onehot, axis=1) - 1
    position = lax.optimization_barrier(jnp.sum(running * onehot, axis=2))
    sources = jnp.arange(N_EP, dtype=jnp.int32)[:, None]
    return (by_source * (N_EP * CAP) + sources * CAP + position).reshape(TOK).astype(jnp.int32)

def scatter_rows(values, target):
    buffer = jnp.zeros((EXPERTS * N_EP * CAP, D), values.dtype).at[target].set(values)
    return buffer.reshape(EXPERTS, N_EP * CAP, 2, D // 2)

def expert_forward(pieces):
    slots, gate_mat, up_mat, down_mat = pieces
    widened = slots.astype(jnp.float32)
    gate_pre = jnp.einsum('rkd,jkdf->rjf', widened, gate_mat.astype(jnp.float32))
    up_pre = jnp.einsum('rkd,jkdf->rjf', widened, up_mat.astype(jnp.float32))
    hidden = (jax.nn.silu(gate_pre) * up_pre).astype(jnp.bfloat16)
    partial_out = jnp.einsum('rjf,jkfd->rjkd', hidden.astype(jnp.float32), down_mat.astype(jnp.float32)).astype(jnp.bfloat16)
    return lax.optimization_barrier(jnp.sum(partial_out.astype(jnp.float32), axis=1))

def expert_backward(pieces):
    slots, grad_slots, gate_mat, up_mat, down_mat = pieces
    widened = slots.astype(jnp.float32)
    gate_f = gate_mat.astype(jnp.float32)
    up_f = up_mat.astype(jnp.float32)
    gate_pre = jnp.einsum('rkd,jkdf->rjf', widened, gate_f)
    up_pre = jnp.einsum('rkd,jkdf->rjf', widened, up_f)
    grad_hidden = jnp.einsum('rkd,jkfd->rjf', grad_slots.astype(jnp.float32), down_mat.astype(jnp.float32))
    logistic = jax.nn.sigmoid(gate_pre)
    d_gate = (grad_hidden * up_pre * logistic * (1.0 + gate_pre * (1.0 - logistic))).astype(jnp.bfloat16)
    d_up = (grad_hidden * gate_pre * logistic).astype(jnp.bfloat16)
    partial_in = (jnp.einsum('rjf,jkdf->rjkd', d_gate.astype(jnp.float32), gate_f) + jnp.einsum('rjf,jkdf->rjkd', d_up.astype(jnp.float32), up_f)).astype(jnp.bfloat16)
    return lax.optimization_barrier(jnp.sum(partial_in.astype(jnp.float32), axis=1))

def one_section(pieces):
    fwd_rows, fwd_ids, fwd_weight, bwd_rows, bwd_grads, bwd_ids, bwd_weight, norm_scale, gate_blocks, up_blocks, down_blocks = pieces
    gate_mats = gate_blocks.reshape(EXPERTS, SLICES // 2, 2, D // 2, HB)
    up_mats = up_blocks.reshape(EXPERTS, SLICES // 2, 2, D // 2, HB)
    down_mats = down_blocks.reshape(EXPERTS, SLICES // 2, 2, HB, D // 2)
    fwd_normed, fwd_inverse = normalize(fwd_rows, norm_scale)
    fwd_target = build_slots(fwd_ids[:, 0])
    fwd_slots = scatter_rows(fwd_normed, fwd_target)
    fwd_out = lax.map(expert_forward, (fwd_slots, gate_mats, up_mats, down_mats))
    fwd_mixed = fwd_out.reshape(EXPERTS * N_EP * CAP, D)[fwd_target]
    fwd_result = (fwd_rows.astype(jnp.float32) + fwd_weight * fwd_mixed).astype(jnp.bfloat16)
    bwd_normed, bwd_inverse = normalize(bwd_rows, norm_scale)
    weighted = (bwd_weight * bwd_grads.astype(jnp.float32)).astype(jnp.bfloat16)
    bwd_target = build_slots(bwd_ids[:, 0])
    bwd_slots = scatter_rows(bwd_normed, bwd_target)
    grad_slots = scatter_rows(weighted, bwd_target)
    bwd_out = lax.map(expert_backward, (bwd_slots, grad_slots, gate_mats, up_mats, down_mats))
    d_normed = bwd_out.reshape(EXPERTS * N_EP * CAP, D)[bwd_target]
    scaled = norm_scale * d_normed
    widened = bwd_rows.astype(jnp.float32)
    cubed = bwd_inverse * bwd_inverse * bwd_inverse
    d_rows = bwd_grads.astype(jnp.float32) + scaled * bwd_inverse - widened * cubed * lax.optimization_barrier(jnp.mean(scaled * widened, axis=-1, keepdims=True))
    return (fwd_result, d_rows.astype(jnp.bfloat16))

def reference(fwd_act, fwd_route, fwd_gate, bwd_act, bwd_grad, bwd_route, bwd_gate, norm_gain, w_gate, w_up, w_down):
    fwd_all, bwd_all = lax.map(one_section, (fwd_act, fwd_route, fwd_gate, bwd_act, bwd_grad, bwd_route, bwd_gate, norm_gain, w_gate, w_up, w_down))
    return (jnp.roll(fwd_all, 1, axis=0), jnp.roll(bwd_all, -1, axis=0))
```

```python
import functools

import jax
import jax.numpy as jnp
from jax import lax
from jax.experimental import pallas as pl
from jax.experimental.pallas import tpu as pltpu
from jax.sharding import Mesh
from jax.sharding import PartitionSpec as P

EP = ("ep_0", "ep_1", "ep_2")
MESH = pl.DeviceIdType.MESH
BF16, F32 = jnp.bfloat16, jnp.float32
CAP = 10
SLAB = 32
BACK = 16
NT = (((1,), (1,)), ((), ()))


def iota(shape, dim):
    return lax.broadcasted_iota(jnp.int32, shape, dim)


def selector(mask):
    return jnp.where(mask, 1.0, 0.0).astype(BF16)


def dot(a, b):
    return jnp.dot(a, b, preferred_element_type=F32)


def dot_nt(a, b):
    return lax.dot_general(a, b, NT, preferred_element_type=F32)


def aligned(start, size):
    return pl.ds(pl.multiple_of(start, size), size)


def slot_numbers(route):
    count = route.shape[0]
    down, across = iota((count, count), 0), iota((count, count), 1)
    column = route.astype(F32)
    row = jnp.sum(jnp.where(down == across, column, 0.0), axis=0, keepdims=True)
    same = column == row
    row_place = jnp.sum(jnp.where(same & (down < across), 1.0, 0.0), axis=0, keepdims=True)
    column_place = jnp.sum(jnp.where(same & (across < down), 1.0, 0.0), axis=1, keepdims=True)
    return column, column_place, row, row_place


def kernel(
    experts,
    fwd_act,
    fwd_route,
    fwd_gate,
    bwd_act,
    bwd_grad,
    bwd_route,
    bwd_gate,
    gain,
    w_gate,
    w_up,
    w_down,
    fwd_out,
    bwd_out,
    staged,
    outgoing,
    near,
    far,
    rows,
    gate_w,
    up_w,
    down_w,
    pre,
    pre_out,
    pre_in,
    hidden,
    own,
    z_out,
    z_in,
    y_out,
    y_in,
    v_rows,
    results,
    local_sem,
    w_send,
    w_recv,
    a_send,
    a_recv,
    f_send,
    f_recv,
    c_send,
    c_recv,
    z_send,
    z_recv,
    y_send,
    y_recv,
    p_send,
    p_recv,
):
    tokens, width = fwd_act.shape
    half = width // 2
    tile = min(256, half)
    tiles = half // tile
    slabs = 2 * experts
    block = slabs * CAP
    section, y, z, c = (lax.axis_index(a) for a in ("pp", *EP))
    sections = lax.axis_size("pp")
    me = y * 2 + c
    core = 1 - c
    z_weights = z + 1 - 2 * lax.rem(z, 2)
    z_rows = lax.rem(z + 2 * lax.rem(z, 2) + 3, 4)
    following = lax.rem(section + 1, sections)
    previous = lax.rem(section + sections - 1, sections)

    def y_at(step, sign):
        away = (step + 1) // 2 * (2 * lax.rem(step, 2) - 1)
        return lax.rem(y + sign * away + 2 * experts, experts)

    def send(src, dst, sems, index, recv_sems, recv_index, device):
        return pltpu.make_async_remote_copy(
            src_ref=src,
            dst_ref=dst,
            send_sem=sems.at[index],
            recv_sem=recv_sems.at[recv_index],
            device_id=device,
            device_id_type=MESH,
        )

    barrier = pltpu.get_barrier_semaphore()

    def greet(device):
        pl.semaphore_signal(barrier, inc=1, device_id=device, device_id_type=MESH)

    def greet_row(step, _):
        there = y_at(step, 1)
        greet((section, there, z, 0))
        greet((section, there, z, 1))
        return 0

    greet((section, y, z_weights, c))
    greet((section, y, z_rows, c))
    greet((following, y, z, c))
    greet((previous, y, z, c))
    greet((section, y, z, core))
    lax.fori_loop(1, experts, greet_row, 0)

    weights = ((w_gate, gate_w), (w_up, up_w), (w_down, down_w))
    kept = [
        pltpu.make_async_copy(src, dst.at[0], local_sem.at[i])
        for i, (src, dst) in enumerate(weights)
    ]
    for copy in kept:
        copy.start()

    pl.semaphore_wait(barrier, 2 * experts + 3)

    swapped = [
        send(src, dst.at[1], w_send, i, w_recv, i, (section, y, z_weights, c))
        for i, (src, dst) in enumerate(weights)
    ]
    for copy in swapped:
        copy.start()

    def normalized(ref, slot):
        wide = ref[...].astype(F32)
        inverse = lax.rsqrt(jnp.mean(wide * wide, axis=-1, keepdims=True) + 1e-06)
        staged[slot] = (wide * inverse * gain[...]).astype(BF16)
        return inverse

    normalized(fwd_act, 0)
    bwd_inverse = normalized(bwd_act, 1)
    staged[2] = (bwd_gate[...] * bwd_grad[...].astype(F32)).astype(BF16)

    fwd_slots = slot_numbers(fwd_route[...])
    bwd_slots = slot_numbers(bwd_route[...])

    def placing(slots, offset):
        target = (slots[2] * SLAB + slots[3]).astype(jnp.int32) + offset
        return selector(iota((experts * SLAB, tokens), 0) == target)

    place_fwd = placing(fwd_slots, 0)
    place_bwd = placing(bwd_slots, CAP)
    place_grad = placing(bwd_slots, 2 * CAP)

    def place_half(k, _):
        def place_tile(i, _):
            source = aligned(k * half + i * tile, tile)
            placed = dot(place_fwd, staged[0, :, source])
            placed += dot(place_bwd, staged[1, :, source])
            placed += dot(place_grad, staged[2, :, source])
            outgoing[k, :, aligned(i * tile, tile)] = placed.astype(BF16)
            return 0

        return lax.fori_loop(0, tiles, place_tile, 0)

    lax.fori_loop(0, 2, place_half, 0)

    def slab(index):
        return aligned(index * SLAB, SLAB)

    def dispatch(step, k):
        there = y_at(step, 1)
        return send(
            outgoing.at[k, slab(there)],
            near.at[slab(me)],
            a_send,
            step * 2 + k,
            a_recv,
            me,
            (section, there, z, k),
        )

    def dispatch_row(step, _):
        dispatch(step, 0).start()
        dispatch(step, 1).start()
        return 0

    stay = pltpu.make_async_copy(outgoing.at[c, slab(y)], near.at[slab(me)], local_sem.at[3])
    stay.start()
    dispatch(0, core).start()
    lax.fori_loop(1, experts, dispatch_row, 0)

    def arrival(index):
        return send(
            outgoing.at[0, slab(0)],
            near.at[slab(index)],
            a_send,
            0,
            a_recv,
            index,
            (section, y, z, core),
        )

    def forward(index):
        return send(
            near.at[slab(index)],
            far.at[slab(index)],
            f_send,
            index,
            f_recv,
            index,
            (section, y, z_rows, c),
        )

    def forward_row(step, _):
        there = y_at(step, -1) * 2
        for from_core in range(2):
            arrival(there + from_core).wait_recv()
            forward(there + from_core).start()
        return 0

    stay.wait()
    forward(me).start()
    arrival(y * 2 + core).wait_recv()
    forward(y * 2 + core).start()
    lax.fori_loop(1, experts, forward_row, 0)

    source = iota((3 * block, slabs * SLAB), 1)
    within = source & (SLAB - 1)
    kind = (within >= CAP).astype(jnp.int32) + (within >= 2 * CAP).astype(jnp.int32)
    target = kind * block + (source // SLAB) * CAP + within - kind * CAP
    dense = selector(
        (iota((3 * block, slabs * SLAB), 0) == target) & (within < 3 * CAP)
    )

    def take_apart(slab_rows, first):
        def apart(i, _):
            columns = aligned(i * tile, tile)
            values = dot(dense, slab_rows[:, columns]).astype(BF16)
            for kind in range(3):
                rows[kind, first : first + block, columns] = values[
                    kind * block : (kind + 1) * block
                ]
            return 0

        lax.fori_loop(0, tiles, apart, 0)

    take_apart(near, 0)

    def far_arrived(index, _):
        forward(index).wait_recv()
        return 0

    lax.fori_loop(0, slabs, far_arrived, 0)
    take_apart(far, block)

    def first_products(b):
        def of_rows(kind, _):
            for which, weight in ((0, gate_w), (1, up_w)):
                product = dot(rows[kind], weight[b])
                pre[b, 2 * kind + which] = product
                pre_out[b, 2 * kind + which] = product.astype(BF16)
            return 0

        lax.fori_loop(0, 2, of_rows, 0)

    def down_product(b):
        product = dot_nt(rows[2], down_w[b])
        pre[b, 4] = product
        pre_out[b, 4] = product.astype(BF16)

    def cross(b, first, count, index):
        part = pl.ds(first, count)
        return send(
            pre_out.at[b, part],
            pre_in.at[b, part],
            c_send,
            index,
            c_recv,
            index,
            (section, y, z, core),
        )

    def activate(b):
        gate_pre = pre[b, 0] + pre_in[b, 0].astype(F32)
        up_pre = pre[b, 1] + pre_in[b, 1].astype(F32)
        hidden[b, 0] = (gate_pre * jax.nn.sigmoid(gate_pre) * up_pre).astype(BF16)

    def derive(b):
        gate_pre = pre[b, 2] + pre_in[b, 2].astype(F32)
        up_pre = pre[b, 3] + pre_in[b, 3].astype(F32)
        grad = pre[b, 4] + pre_in[b, 4].astype(F32)
        logistic = jax.nn.sigmoid(gate_pre)
        hidden[b, 1] = (
            grad * up_pre * logistic * (1.0 + gate_pre * (1.0 - logistic))
        ).astype(BF16)
        hidden[b, 2] = (grad * gate_pre * logistic).astype(BF16)

    for copy in kept:
        copy.wait()
    first_products(0)
    down_product(0)
    cross(0, 0, 5, 0).start()

    swapped[0].wait_recv()
    swapped[1].wait_recv()
    first_products(1)
    cross(1, 0, 4, 1).start()
    cross(0, 0, 5, 0).wait_recv()
    activate(0)
    derive(0)
    cross(1, 0, 4, 1).wait_recv()
    activate(1)

    swapped[2].wait_recv()
    down_product(1)
    cross(1, 4, 1, 2).start()

    def give_back(which):
        return send(
            z_out.at[which], z_in.at[which], z_send, which, z_recv, which, (section, y, z_rows, c)
        )

    def split(which, columns, values):
        own[which, :, columns] = values[:block]
        z_out[which, :, columns] = values[block:].astype(BF16)

    def forward_tile(i, _):
        columns = aligned(i * tile, tile)
        split(
            0,
            columns,
            dot(hidden[0, 0], down_w[0, :, columns]) + dot(hidden[1, 0], down_w[1, :, columns]),
        )
        return 0

    lax.fori_loop(0, tiles, forward_tile, 0)
    give_back(0).start()

    cross(1, 4, 1, 2).wait_recv()
    derive(1)

    def backward_tile(i, _):
        columns = aligned(i * tile, tile)
        values = dot_nt(hidden[0, 1], gate_w[0, columns, :])
        values += dot_nt(hidden[1, 1], gate_w[1, columns, :])
        values += dot_nt(hidden[0, 2], up_w[0, columns, :])
        values += dot_nt(hidden[1, 2], up_w[1, columns, :])
        split(1, columns, values)
        return 0

    lax.fori_loop(0, tiles, backward_tile, 0)
    give_back(1).start()

    back = iota((slabs * BACK, block), 0)
    place = back & (BACK - 1)
    spread = selector(
        (iota((slabs * BACK, block), 1) == (back // BACK) * CAP + place) & (place < CAP)
    )

    def slots_of(index):
        return aligned(index * BACK, BACK)

    def returning(which, step, to_core):
        there = y_at(step, 1)
        return send(
            y_out.at[which, slots_of(there * 2 + to_core)],
            y_in.at[which, c, slots_of(y)],
            y_send.at[which],
            step * 2 + to_core,
            y_recv.at[which],
            y * 2 + c,
            (section, there, z, to_core),
        )

    def staying(which):
        return pltpu.make_async_copy(
            y_out.at[which, slots_of(me)],
            y_in.at[which, c, slots_of(y)],
            local_sem.at[4 + which],
        )

    def send_back(which):
        give_back(which).wait_recv()

        def spread_tile(i, _):
            columns = aligned(i * tile, tile)
            total = (own[which, :, columns] + z_in[which, :, columns].astype(F32)).astype(BF16)
            y_out[which, :, columns] = dot(spread, total).astype(BF16)
            return 0

        lax.fori_loop(0, tiles, spread_tile, 0)

        def return_row(step, _):
            returning(which, step, 0).start()
            returning(which, step, 1).start()
            return 0

        staying(which).start()
        returning(which, 0, core).start()
        lax.fori_loop(1, experts, return_row, 0)

    def returned(which, index, k, e):
        return send(
            y_out.at[which, slots_of(0)],
            y_in.at[which, k, slots_of(e)],
            y_send.at[which],
            0,
            y_recv.at[which],
            index,
            (section, y, z, core),
        )

    def collect(which):
        def from_row(step, _):
            there = y_at(step, -1)
            returned(which, there * 2, 0, there).wait_recv()
            returned(which, there * 2 + 1, 1, there).wait_recv()
            return 0

        staying(which).wait()
        returned(which, y * 2 + core, core, y).wait_recv()
        lax.fori_loop(1, experts, from_row, 0)

    send_back(0)
    send_back(1)

    def picking(slots):
        target = (slots[0] * BACK + slots[1]).astype(jnp.int32)
        return selector(iota((tokens, experts * BACK), 1) == target)

    collect(0)
    pick_fwd = picking(fwd_slots)

    def forward_half(k, _):
        def finish(i, _):
            columns = aligned(k * half + i * tile, tile)
            mixed = dot(pick_fwd, y_in[0, k, :, aligned(i * tile, tile)])
            results[0, :, columns] = (
                fwd_act[:, columns].astype(F32) + fwd_gate[...] * mixed
            ).astype(BF16)
            return 0

        return lax.fori_loop(0, tiles, finish, 0)

    lax.fori_loop(0, 2, forward_half, 0)
    to_next = send(results.at[0], fwd_out, p_send, 0, p_recv, 0, (following, y, z, c))
    to_next.start()

    collect(1)
    pick_bwd = picking(bwd_slots)

    def gather_half(k, dotted):
        def gather(i, dotted):
            columns = aligned(k * half + i * tile, tile)
            scaled = gain[:, columns] * dot(pick_bwd, y_in[1, k, :, aligned(i * tile, tile)])
            v_rows[:, columns] = scaled
            return dotted + scaled * bwd_act[:, columns].astype(F32)

        return lax.fori_loop(0, tiles, gather, dotted)

    dotted = lax.fori_loop(0, 2, gather_half, jnp.zeros((tokens, tile), F32))
    mean = jnp.sum(dotted, axis=-1, keepdims=True) / width
    factor = bwd_inverse * bwd_inverse * bwd_inverse * mean

    def backward_finish(i, _):
        columns = aligned(i * tile, tile)
        results[1, :, columns] = (
            bwd_grad[:, columns].astype(F32)
            + v_rows[:, columns] * bwd_inverse
            - bwd_act[:, columns].astype(F32) * factor
        ).astype(BF16)
        return 0

    lax.fori_loop(0, 2 * tiles, backward_finish, 0)
    to_previous = send(results.at[1], bwd_out, p_send, 1, p_recv, 1, (previous, y, z, c))
    to_previous.start()

    for copy in swapped:
        copy.wait_send()
    dispatch(0, core).wait_send()
    returning(0, 0, core).wait_send()
    returning(1, 0, core).wait_send()

    def row_left(step, _):
        for k in range(2):
            dispatch(step, k).wait_send()
            returning(0, step, k).wait_send()
            returning(1, step, k).wait_send()
        return 0

    lax.fori_loop(1, experts, row_left, 0)

    def forward_left(index, _):
        forward(index).wait_send()
        return 0

    lax.fori_loop(0, slabs, forward_left, 0)
    cross(0, 0, 5, 0).wait_send()
    cross(1, 0, 4, 1).wait_send()
    cross(1, 4, 1, 2).wait_send()
    give_back(0).wait_send()
    give_back(1).wait_send()
    to_next.wait()
    to_previous.wait()


def body(
    fwd_act,
    fwd_route,
    fwd_gate,
    bwd_act,
    bwd_grad,
    bwd_route,
    bwd_gate,
    norm_gain,
    w_gate,
    w_up,
    w_down,
):
    experts = lax.axis_size("ep_0")
    _, tokens, width = fwd_act.shape
    _, _, half, units = w_gate.shape
    slabs = 2 * experts
    block = slabs * CAP
    dma = pltpu.SemaphoreType.DMA
    vmem = pl.BlockSpec(memory_space=pltpu.VMEM)
    anywhere = pl.BlockSpec(memory_space=pl.ANY)
    outs = pl.pallas_call(
        functools.partial(kernel, experts),
        out_shape=[jax.ShapeDtypeStruct((tokens, width), BF16)] * 2,
        in_specs=[vmem] * 8 + [anywhere] * 3,
        out_specs=[vmem] * 2,
        scratch_shapes=[
            pltpu.VMEM((3, tokens, width), BF16),
            pltpu.VMEM((2, experts * SLAB, half), BF16),
            pltpu.VMEM((slabs * SLAB, half), BF16),
            pltpu.VMEM((slabs * SLAB, half), BF16),
            pltpu.VMEM((3, 2 * block, half), BF16),
            pltpu.VMEM((2, half, units), BF16),
            pltpu.VMEM((2, half, units), BF16),
            pltpu.VMEM((2, units, half), BF16),
            pltpu.VMEM((2, 5, 2 * block, units), F32),
            pltpu.VMEM((2, 5, 2 * block, units), BF16),
            pltpu.VMEM((2, 5, 2 * block, units), BF16),
            pltpu.VMEM((2, 3, 2 * block, units), BF16),
            pltpu.VMEM((2, block, half), F32),
            pltpu.VMEM((2, block, half), BF16),
            pltpu.VMEM((2, block, half), BF16),
            pltpu.VMEM((2, slabs * BACK, half), BF16),
            pltpu.VMEM((2, 2, experts * BACK, half), BF16),
            pltpu.VMEM((tokens, width), F32),
            pltpu.VMEM((2, tokens, width), BF16),
            dma((6,)),
            dma((3,)),
            dma((3,)),
            dma((slabs,)),
            dma((slabs,)),
            dma((slabs,)),
            dma((slabs,)),
            dma((3,)),
            dma((3,)),
            dma((2,)),
            dma((2,)),
            dma((2, slabs)),
            dma((2, slabs)),
            dma((2,)),
            dma((2,)),
        ],
        compiler_params=pltpu.CompilerParams(
            collective_id=0, has_side_effects=True, vmem_limit_bytes=60 * 1024 * 1024
        ),
        name="relay_layer",
    )(
        fwd_act[0],
        fwd_route[0],
        fwd_gate[0],
        bwd_act[0],
        bwd_grad[0],
        bwd_route[0],
        bwd_gate[0],
        norm_gain,
        w_gate[0, 0],
        w_up[0, 0],
        w_down[0, 0],
    )
    return tuple(out[None] for out in outs)


def solution(mesh):
    sections = mesh.shape["pp"]
    split = Mesh(
        mesh.devices.reshape(sections, mesh.shape["ep"] // 8, 4, 2), ("pp", "ep_0", "ep_1", "ep_2")
    )
    rows = P("pp", EP, None)
    weights = P("pp", EP, None, None)
    return jax.shard_map(
        body,
        mesh=split,
        in_specs=(rows,) * 7 + (P("pp", None),) + (weights,) * 3,
        out_specs=(rows, rows),
        check_vma=False,
    )
```

```python
import functools

import jax
import jax.numpy as jnp
from jax import lax
from jax.experimental import pallas as pl
from jax.experimental.pallas import tpu as pltpu
from jax.sharding import Mesh
from jax.sharding import PartitionSpec as P

EP = ("ep_0", "ep_1", "ep_2")
MESH = pl.DeviceIdType.MESH
BF16, F32 = jnp.bfloat16, jnp.float32
CAP = 10
SLAB = 32
BACK = 16
NT = (((1,), (1,)), ((), ()))
PIECES = ((0, 2), (2, 3), (5, 2))
DETOUR = 80


def iota(shape, dim):
    return lax.broadcasted_iota(jnp.int32, shape, dim)


def selector(mask):
    return jnp.where(mask, 1.0, 0.0).astype(BF16)


def dot(a, b):
    return jnp.dot(a, b, preferred_element_type=F32)


def dot_nt(a, b):
    return lax.dot_general(a, b, NT, preferred_element_type=F32)


def aligned(start, size):
    return pl.ds(pl.multiple_of(start, size), size)


def as_column(row):
    count = row.shape[1]
    mine = iota((count, count), 0) == iota((count, count), 1)
    return jnp.sum(jnp.where(mine, row, 0.0), axis=1, keepdims=True)


def slot_numbers(route):
    count = route.shape[1]
    down, across = iota((count, count), 0), iota((count, count), 1)
    row = route.astype(F32)
    column = as_column(row)
    same = column == row
    row_place = jnp.sum(jnp.where(same & (down < across), 1.0, 0.0), axis=0, keepdims=True)
    column_place = jnp.sum(jnp.where(same & (across < down), 1.0, 0.0), axis=1, keepdims=True)
    return column, column_place, row, row_place


def kernel(
    experts,
    fwd_act,
    fwd_route,
    fwd_gate,
    bwd_act,
    bwd_grad,
    bwd_route,
    bwd_gate,
    gain,
    w_gate,
    w_up,
    w_down,
    fwd_out,
    bwd_out,
    staged,
    outgoing,
    near,
    far,
    rows,
    gate_w,
    up_w,
    down_w,
    pre,
    pre_out,
    pre_in,
    hidden,
    own,
    z_out,
    z_in,
    y_out,
    y_in,
    v_rows,
    results,
    passing_w,
    passing_z,
    local_sem,
    w_send,
    w_recv,
    a_send,
    a_recv,
    f_send,
    f_recv,
    c_send,
    c_recv,
    z_send,
    z_recv,
    y_send,
    y_recv,
    p_send,
    p_recv,
    d_send,
    d_recv,
):
    tokens, width = fwd_act.shape
    half = width // 2
    tile = min(256, half)
    tiles = half // tile
    slabs = 2 * experts
    block = slabs * CAP
    section, y, z, c = (lax.axis_index(a) for a in ("pp", *EP))
    sections = lax.axis_size("pp")
    me = y * 2 + c
    core = 1 - c
    odd_column = lax.rem(section // 2, 2)
    turn = 2 * lax.rem(z + odd_column, 2)
    z_weights = lax.rem(z + 5 - turn, 4)
    z_rows = lax.rem(z + 3 + turn, 4)
    beside = section + 2 - 4 * odd_column
    following = lax.rem(section + 1, sections)
    previous = lax.rem(section + sections - 1, sections)

    def y_at(step, sign):
        away = (step + 1) // 2 * (2 * lax.rem(step, 2) - 1)
        return lax.rem(y + sign * away + 2 * experts, experts)

    def send(src, dst, sems, index, recv_sems, recv_index, device):
        return pltpu.make_async_remote_copy(
            src_ref=src,
            dst_ref=dst,
            send_sem=sems.at[index],
            recv_sem=recv_sems.at[recv_index],
            device_id=device,
            device_id_type=MESH,
        )

    barrier = pltpu.get_barrier_semaphore()

    def greet(device):
        pl.semaphore_signal(barrier, inc=1, device_id=device, device_id_type=MESH)

    def greet_row(step, _):
        there = y_at(step, 1)
        greet((section, there, z, 0))
        greet((section, there, z, 1))
        return 0

    greet((section, y, z_weights, c))
    greet((section, y, z_rows, c))
    greet((beside, y, z, c))
    greet((following, y, z, c))
    greet((previous, y, z, c))
    greet((section, y, z, core))
    lax.fori_loop(1, experts, greet_row, 0)

    weights = ((w_gate, gate_w), (w_up, up_w), (w_down, down_w))
    kept = [
        pltpu.make_async_copy(src, dst.at[0], local_sem.at[i])
        for i, (src, dst) in enumerate(weights)
    ]
    for copy in kept:
        copy.start()

    pl.semaphore_wait(barrier, 2 * experts + 4)

    units = w_down.shape[0] - DETOUR
    pieces = PIECES

    def piece_columns(piece):
        start, count = pieces[piece]
        return pl.ds(start * tile, count * tile)

    def detour(which, step):
        if which == 2:
            stops = (
                w_down.at[pl.ds(units, DETOUR)],
                passing_w.at[0],
                passing_w.at[1],
                down_w.at[1, pl.ds(units, DETOUR)],
            )
        else:
            columns = piece_columns(0)
            stops = (
                z_out.at[which, :, columns],
                passing_z.at[0, which],
                passing_z.at[1, which],
                z_in.at[which, :, columns],
            )
        along_z = (section, y, z_rows if which == 2 else z_weights, c)
        return send(
            stops[step],
            stops[step + 1],
            d_send,
            which * 3 + step,
            d_recv,
            which * 3 + step,
            along_z if step == 1 else (beside, y, z, c),
        )

    detour(2, 0).start()
    swaps = (
        (w_gate, gate_w.at[1]),
        (w_up, up_w.at[1]),
        (w_down.at[pl.ds(0, units)], down_w.at[1, pl.ds(0, units)]),
    )
    swapped = [
        send(src, dst, w_send, i, w_recv, i, (section, y, z_weights, c))
        for i, (src, dst) in enumerate(swaps)
    ]
    for copy in swapped:
        copy.start()

    def normalized(ref, slot):
        wide = ref[...].astype(F32)
        inverse = lax.rsqrt(jnp.mean(wide * wide, axis=-1, keepdims=True) + 1e-06)
        staged[slot] = (wide * inverse * gain[...]).astype(BF16)
        return inverse

    normalized(fwd_act, 0)
    bwd_inverse = normalized(bwd_act, 1)
    staged[2] = (as_column(bwd_gate[...]) * bwd_grad[...].astype(F32)).astype(BF16)

    fwd_slots = slot_numbers(fwd_route[...])
    bwd_slots = slot_numbers(bwd_route[...])

    def placing(slots, offset):
        target = (slots[2] * SLAB + slots[3]).astype(jnp.int32) + offset
        return selector(iota((experts * SLAB, tokens), 0) == target)

    place_fwd = placing(fwd_slots, 0)
    place_bwd = placing(bwd_slots, CAP)
    place_grad = placing(bwd_slots, 2 * CAP)

    def place_half(k, _):
        def place_tile(i, _):
            source = aligned(k * half + i * tile, tile)
            placed = dot(place_fwd, staged[0, :, source])
            placed += dot(place_bwd, staged[1, :, source])
            placed += dot(place_grad, staged[2, :, source])
            outgoing[k, :, aligned(i * tile, tile)] = placed.astype(BF16)
            return 0

        return lax.fori_loop(0, tiles, place_tile, 0)

    lax.fori_loop(0, 2, place_half, 0)

    def slab(index):
        return aligned(index * SLAB, SLAB)

    def dispatch(step, k):
        there = y_at(step, 1)
        return send(
            outgoing.at[k, slab(there)],
            near.at[slab(me)],
            a_send,
            step * 2 + k,
            a_recv,
            me,
            (section, there, z, k),
        )

    def dispatch_row(step, _):
        dispatch(step, 0).start()
        dispatch(step, 1).start()
        return 0

    stay = pltpu.make_async_copy(outgoing.at[c, slab(y)], near.at[slab(me)], local_sem.at[3])
    stay.start()
    dispatch(0, core).start()
    lax.fori_loop(1, experts, dispatch_row, 0)
    detour(2, 0).wait_recv()
    detour(2, 1).start()

    def arrival(index):
        return send(
            outgoing.at[0, slab(0)],
            near.at[slab(index)],
            a_send,
            0,
            a_recv,
            index,
            (section, y, z, core),
        )

    def forward(index):
        return send(
            near.at[slab(index)],
            far.at[slab(index)],
            f_send,
            index,
            f_recv,
            index,
            (section, y, z_rows, c),
        )

    def forward_row(step, _):
        there = y_at(step, -1) * 2
        for from_core in range(2):
            arrival(there + from_core).wait_recv()
            forward(there + from_core).start()
        return 0

    stay.wait()
    forward(me).start()
    arrival(y * 2 + core).wait_recv()
    forward(y * 2 + core).start()
    lax.fori_loop(1, experts, forward_row, 0)

    source = iota((3 * block, slabs * SLAB), 1)
    within = source & (SLAB - 1)
    kind = (within >= CAP).astype(jnp.int32) + (within >= 2 * CAP).astype(jnp.int32)
    target = kind * block + (source // SLAB) * CAP + within - kind * CAP
    dense = selector(
        (iota((3 * block, slabs * SLAB), 0) == target) & (within < 3 * CAP)
    )

    def take_apart(slab_rows, first):
        def apart(i, _):
            columns = aligned(i * tile, tile)
            values = dot(dense, slab_rows[:, columns]).astype(BF16)
            for kind in range(3):
                rows[kind, first : first + block, columns] = values[
                    kind * block : (kind + 1) * block
                ]
            return 0

        lax.fori_loop(0, tiles, apart, 0)

    take_apart(near, 0)
    detour(2, 1).wait_recv()
    detour(2, 2).start()

    def far_arrived(index, _):
        forward(index).wait_recv()
        return 0

    lax.fori_loop(0, slabs, far_arrived, 0)
    take_apart(far, block)

    def first_products(b):
        def of_rows(kind, _):
            for which, weight in ((0, gate_w), (1, up_w)):
                product = dot(rows[kind], weight[b])
                pre[b, 2 * kind + which] = product
                pre_out[b, 2 * kind + which] = product.astype(BF16)
            return 0

        lax.fori_loop(0, 2, of_rows, 0)

    def down_product(b):
        product = dot_nt(rows[2], down_w[b])
        pre[b, 4] = product
        pre_out[b, 4] = product.astype(BF16)

    def cross(b, first, count, index):
        part = pl.ds(first, count)
        return send(
            pre_out.at[b, part],
            pre_in.at[b, part],
            c_send,
            index,
            c_recv,
            index,
            (section, y, z, core),
        )

    def activate(b):
        gate_pre = pre[b, 0] + pre_in[b, 0].astype(F32)
        up_pre = pre[b, 1] + pre_in[b, 1].astype(F32)
        hidden[b, 0] = (gate_pre * jax.nn.sigmoid(gate_pre) * up_pre).astype(BF16)

    def derive(b):
        gate_pre = pre[b, 2] + pre_in[b, 2].astype(F32)
        up_pre = pre[b, 3] + pre_in[b, 3].astype(F32)
        grad = pre[b, 4] + pre_in[b, 4].astype(F32)
        logistic = jax.nn.sigmoid(gate_pre)
        hidden[b, 1] = (
            grad * up_pre * logistic * (1.0 + gate_pre * (1.0 - logistic))
        ).astype(BF16)
        hidden[b, 2] = (grad * gate_pre * logistic).astype(BF16)

    for copy in kept:
        copy.wait()
    first_products(0)
    down_product(0)
    cross(0, 0, 5, 0).start()

    swapped[0].wait_recv()
    swapped[1].wait_recv()
    first_products(1)
    cross(1, 0, 4, 1).start()
    cross(0, 0, 5, 0).wait_recv()
    activate(0)
    derive(0)
    cross(1, 0, 4, 1).wait_recv()
    activate(1)

    swapped[2].wait_recv()
    detour(2, 2).wait_recv()
    down_product(1)
    cross(1, 4, 1, 2).start()

    def give_back(which, piece):
        columns = piece_columns(piece)
        return send(
            z_out.at[which, :, columns],
            z_in.at[which, :, columns],
            z_send.at[which],
            piece,
            z_recv.at[which],
            piece,
            (section, y, z_rows, c),
        )

    def give_back_all(which, one_tile):
        for piece, (start, count) in enumerate(pieces):
            lax.fori_loop(start, start + count, one_tile, 0)
            if piece == 0:
                detour(which, 0).start()
            else:
                give_back(which, piece).start()

    def split(which, columns, values):
        own[which, :, columns] = values[:block]
        z_out[which, :, columns] = values[block:].astype(BF16)

    def forward_tile(i, _):
        columns = aligned(i * tile, tile)
        split(
            0,
            columns,
            dot(hidden[0, 0], down_w[0, :, columns]) + dot(hidden[1, 0], down_w[1, :, columns]),
        )
        return 0

    give_back_all(0, forward_tile)

    cross(1, 4, 1, 2).wait_recv()
    derive(1)

    def backward_tile(i, _):
        columns = aligned(i * tile, tile)
        values = dot_nt(hidden[0, 1], gate_w[0, columns, :])
        values += dot_nt(hidden[1, 1], gate_w[1, columns, :])
        values += dot_nt(hidden[0, 2], up_w[0, columns, :])
        values += dot_nt(hidden[1, 2], up_w[1, columns, :])
        split(1, columns, values)
        return 0

    give_back_all(1, backward_tile)

    back = iota((slabs * BACK, block), 0)
    place = back & (BACK - 1)
    spread = selector(
        (iota((slabs * BACK, block), 1) == (back // BACK) * CAP + place) & (place < CAP)
    )

    def slots_of(index):
        return aligned(index * BACK, BACK)

    def returning(which, piece, step, to_core):
        there = y_at(step, 1)
        columns = piece_columns(piece)
        return send(
            y_out.at[which, slots_of(there * 2 + to_core), columns],
            y_in.at[which, c, slots_of(y), columns],
            y_send.at[which, piece],
            step * 2 + to_core,
            y_recv.at[which, piece],
            y * 2 + c,
            (section, there, z, to_core),
        )

    def staying(which, piece):
        columns = piece_columns(piece)
        return pltpu.make_async_copy(
            y_out.at[which, slots_of(me), columns],
            y_in.at[which, c, slots_of(y), columns],
            local_sem.at[4 + which * len(PIECES) + piece],
        )

    def send_back(which, piece):
        if piece == 0:
            detour(which, 2).wait_recv()
        else:
            give_back(which, piece).wait_recv()
        first, count = pieces[piece]

        def spread_tile(i, _):
            columns = aligned(i * tile, tile)
            total = (own[which, :, columns] + z_in[which, :, columns].astype(F32)).astype(BF16)
            y_out[which, :, columns] = dot(spread, total).astype(BF16)
            return 0

        lax.fori_loop(first, first + count, spread_tile, 0)

        def return_row(step, _):
            returning(which, piece, step, 0).start()
            returning(which, piece, step, 1).start()
            return 0

        staying(which, piece).start()
        returning(which, piece, 0, core).start()
        lax.fori_loop(1, experts, return_row, 0)

    def returned(which, piece, k, e):
        columns = piece_columns(piece)
        return send(
            y_out.at[which, slots_of(0), columns],
            y_in.at[which, k, slots_of(e), columns],
            y_send.at[which, piece],
            0,
            y_recv.at[which, piece],
            e * 2 + k,
            (section, y, z, core),
        )

    def collect(which, piece):
        def from_row(step, _):
            there = y_at(step, -1)
            returned(which, piece, 0, there).wait_recv()
            returned(which, piece, 1, there).wait_recv()
            return 0

        staying(which, piece).wait()
        returned(which, piece, core, y).wait_recv()
        lax.fori_loop(1, experts, from_row, 0)

    detour(0, 0).wait_recv()
    detour(0, 1).start()
    detour(1, 0).wait_recv()
    detour(1, 1).start()
    send_back(0, 1)
    detour(0, 1).wait_recv()
    detour(0, 2).start()
    send_back(0, 2)
    send_back(0, 0)
    detour(1, 1).wait_recv()
    detour(1, 2).start()
    for piece in range(len(pieces)):
        send_back(1, piece)

    def picking(slots):
        target = (slots[0] * BACK + slots[1]).astype(jnp.int32)
        return selector(iota((tokens, experts * BACK), 1) == target)

    pick_fwd = picking(fwd_slots)
    fwd_scale = as_column(fwd_gate[...])
    for piece in (1, 2, 0):
        start, count = pieces[piece]
        collect(0, piece)
        for k in range(2):

            def finish(i, _):
                columns = aligned(k * half + i * tile, tile)
                mixed = dot(pick_fwd, y_in[0, k, :, aligned(i * tile, tile)])
                results[0, :, columns] = (
                    fwd_act[:, columns].astype(F32) + fwd_scale * mixed
                ).astype(BF16)
                return 0

            lax.fori_loop(start, start + count, finish, 0)
    to_next = send(results.at[0], fwd_out, p_send, 0, p_recv, 0, (following, y, z, c))
    to_next.start()

    pick_bwd = picking(bwd_slots)
    dotted = jnp.zeros((tokens, tile), F32)
    for piece, (start, count) in enumerate(pieces):
        collect(1, piece)
        for k in range(2):

            def gather(i, dotted):
                columns = aligned(k * half + i * tile, tile)
                scaled = gain[:, columns] * dot(pick_bwd, y_in[1, k, :, aligned(i * tile, tile)])
                v_rows[:, columns] = scaled
                return dotted + scaled * bwd_act[:, columns].astype(F32)

            dotted = lax.fori_loop(start, start + count, gather, dotted)
    mean = jnp.sum(dotted, axis=-1, keepdims=True) / width
    factor = bwd_inverse * bwd_inverse * bwd_inverse * mean

    def backward_finish(i, _):
        columns = aligned(i * tile, tile)
        results[1, :, columns] = (
            bwd_grad[:, columns].astype(F32)
            + v_rows[:, columns] * bwd_inverse
            - bwd_act[:, columns].astype(F32) * factor
        ).astype(BF16)
        return 0

    lax.fori_loop(0, 2 * tiles, backward_finish, 0)
    to_previous = send(results.at[1], bwd_out, p_send, 1, p_recv, 1, (previous, y, z, c))
    to_previous.start()

    for copy in swapped:
        copy.wait_send()
    for which in range(3):
        for step in range(3):
            detour(which, step).wait_send()
    dispatch(0, core).wait_send()
    for which in range(2):
        for piece in range(len(pieces)):
            returning(which, piece, 0, core).wait_send()
            if piece:
                give_back(which, piece).wait_send()

    def row_left(step, _):
        for k in range(2):
            dispatch(step, k).wait_send()
            for which in range(2):
                for piece in range(len(pieces)):
                    returning(which, piece, step, k).wait_send()
        return 0

    lax.fori_loop(1, experts, row_left, 0)

    def forward_left(index, _):
        forward(index).wait_send()
        return 0

    lax.fori_loop(0, slabs, forward_left, 0)
    cross(0, 0, 5, 0).wait_send()
    cross(1, 0, 4, 1).wait_send()
    cross(1, 4, 1, 2).wait_send()
    to_next.wait()
    to_previous.wait()


def body(
    fwd_act,
    fwd_route,
    fwd_gate,
    bwd_act,
    bwd_grad,
    bwd_route,
    bwd_gate,
    norm_gain,
    w_gate,
    w_up,
    w_down,
):
    experts = lax.axis_size("ep_0")
    _, tokens, width = fwd_act.shape
    _, _, half, units = w_gate.shape
    slabs = 2 * experts
    block = slabs * CAP
    dma = pltpu.SemaphoreType.DMA
    vmem = pl.BlockSpec(memory_space=pltpu.VMEM)
    anywhere = pl.BlockSpec(memory_space=pl.ANY)
    outs = pl.pallas_call(
        functools.partial(kernel, experts),
        out_shape=[jax.ShapeDtypeStruct((tokens, width), BF16)] * 2,
        in_specs=[vmem] * 8 + [anywhere] * 3,
        out_specs=[vmem] * 2,
        scratch_shapes=[
            pltpu.VMEM((3, tokens, width), BF16),
            pltpu.VMEM((2, experts * SLAB, half), BF16),
            pltpu.VMEM((slabs * SLAB, half), BF16),
            pltpu.VMEM((slabs * SLAB, half), BF16),
            pltpu.VMEM((3, 2 * block, half), BF16),
            pltpu.VMEM((2, half, units), BF16),
            pltpu.VMEM((2, half, units), BF16),
            pltpu.VMEM((2, units, half), BF16),
            pltpu.VMEM((2, 5, 2 * block, units), F32),
            pltpu.VMEM((2, 5, 2 * block, units), BF16),
            pltpu.VMEM((2, 5, 2 * block, units), BF16),
            pltpu.VMEM((2, 3, 2 * block, units), BF16),
            pltpu.VMEM((2, block, half), F32),
            pltpu.VMEM((2, block, half), BF16),
            pltpu.VMEM((2, block, half), BF16),
            pltpu.VMEM((2, slabs * BACK, half), BF16),
            pltpu.VMEM((2, 2, experts * BACK, half), BF16),
            pltpu.VMEM((tokens, width), F32),
            pltpu.VMEM((2, tokens, width), BF16),
            pltpu.VMEM((2, DETOUR, half), BF16),
            pltpu.VMEM((2, 2, block, PIECES[0][1] * 256), BF16),
            dma((4 + 2 * len(PIECES),)),
            dma((3,)),
            dma((3,)),
            dma((slabs,)),
            dma((slabs,)),
            dma((slabs,)),
            dma((slabs,)),
            dma((3,)),
            dma((3,)),
            dma((2, len(PIECES))),
            dma((2, len(PIECES))),
            dma((2, len(PIECES), slabs)),
            dma((2, len(PIECES), slabs)),
            dma((2,)),
            dma((2,)),
            dma((9,)),
            dma((9,)),
        ],
        compiler_params=pltpu.CompilerParams(
            collective_id=0, has_side_effects=True, vmem_limit_bytes=60 * 1024 * 1024
        ),
        name="relay_layer",
    )(
        fwd_act[0],
        fwd_route[:, :, 0],
        fwd_gate[:, :, 0],
        bwd_act[0],
        bwd_grad[0],
        bwd_route[:, :, 0],
        bwd_gate[:, :, 0],
        norm_gain,
        w_gate[0, 0],
        w_up[0, 0],
        w_down[0, 0],
    )
    return tuple(out[None] for out in outs)


def solution(mesh):
    sections = mesh.shape["pp"]
    split = Mesh(
        mesh.devices.reshape(sections, mesh.shape["ep"] // 8, 4, 2), ("pp", "ep_0", "ep_1", "ep_2")
    )
    rows = P("pp", EP, None)
    weights = P("pp", EP, None, None)
    return jax.shard_map(
        body,
        mesh=split,
        in_specs=(rows,) * 7 + (P("pp", None),) + (weights,) * 3,
        out_specs=(rows, rows),
        check_vma=False,
    )
```

```python
import functools

import jax
import jax.numpy as jnp
from jax import lax
from jax.experimental import pallas as pl
from jax.experimental.pallas import tpu as pltpu
from jax.sharding import Mesh
from jax.sharding import PartitionSpec as P

EP = ("ep_0", "ep_1", "ep_2")
MESH = pl.DeviceIdType.MESH
BF16, F32 = jnp.bfloat16, jnp.float32
CAP = 10
SLAB = 32
BACK = 16
NT = (((1,), (1,)), ((), ()))
PIECES = ((0, 2), (2, 3), (5, 2))
DETOUR = 80


def iota(shape, dim):
    return lax.broadcasted_iota(jnp.int32, shape, dim)


def selector(mask):
    return jnp.where(mask, 1.0, 0.0).astype(BF16)


def dot(a, b):
    return jnp.dot(a, b, preferred_element_type=F32)


def dot_nt(a, b):
    return lax.dot_general(a, b, NT, preferred_element_type=F32)


def aligned(start, size):
    return pl.ds(pl.multiple_of(start, size), size)


def as_column(row):
    count = row.shape[1]
    mine = iota((count, count), 0) == iota((count, count), 1)
    return jnp.sum(jnp.where(mine, row, 0.0), axis=1, keepdims=True)


def slot_numbers(route):
    count = route.shape[1]
    down, across = iota((count, count), 0), iota((count, count), 1)
    row = route.astype(F32)
    column = as_column(row)
    same = column == row
    row_place = jnp.sum(jnp.where(same & (down < across), 1.0, 0.0), axis=0, keepdims=True)
    column_place = jnp.sum(jnp.where(same & (across < down), 1.0, 0.0), axis=1, keepdims=True)
    return column, column_place, row, row_place


def kernel(
    experts,
    fwd_act,
    fwd_route,
    fwd_gate,
    bwd_act,
    bwd_grad,
    bwd_route,
    bwd_gate,
    gain,
    w_gate,
    w_up,
    w_down,
    fwd_out,
    bwd_out,
    staged,
    outgoing,
    near,
    far,
    rows,
    gate_w,
    up_w,
    down_w,
    pre,
    pre_out,
    pre_in,
    hidden,
    own,
    z_out,
    z_in,
    y_out,
    y_in,
    v_rows,
    results,
    passing_w,
    passing_z,
    local_sem,
    w_send,
    w_recv,
    a_send,
    a_recv,
    f_send,
    f_recv,
    c_send,
    c_recv,
    z_send,
    z_recv,
    y_send,
    y_recv,
    p_send,
    p_recv,
    d_send,
    d_recv,
):
    tokens, width = fwd_act.shape
    half = width // 2
    tile = min(256, half)
    tiles = half // tile
    slabs = 2 * experts
    block = slabs * CAP
    section, y, z, c = (lax.axis_index(a) for a in ("pp", *EP))
    sections = lax.axis_size("pp")
    me = y * 2 + c
    core = 1 - c
    odd_column = lax.rem(section // 2, 2)
    turn = 2 * lax.rem(z + odd_column, 2)
    z_weights = lax.rem(z + 5 - turn, 4)
    z_rows = lax.rem(z + 3 + turn, 4)
    beside = section + 2 - 4 * odd_column
    following = lax.rem(section + 1, sections)
    previous = lax.rem(section + sections - 1, sections)

    def y_at(step, sign):
        away = (step + 1) // 2 * (2 * lax.rem(step, 2) - 1)
        return lax.rem(y + sign * away + 2 * experts, experts)

    def send(src, dst, sems, index, recv_sems, recv_index, device):
        return pltpu.make_async_remote_copy(
            src_ref=src,
            dst_ref=dst,
            send_sem=sems.at[index],
            recv_sem=recv_sems.at[recv_index],
            device_id=device,
            device_id_type=MESH,
        )

    barrier = pltpu.get_barrier_semaphore()

    def greet(device):
        pl.semaphore_signal(barrier, inc=1, device_id=device, device_id_type=MESH)

    def greet_row(step, _):
        there = y_at(step, 1)
        greet((section, there, z, 0))
        greet((section, there, z, 1))
        return 0

    greet((section, y, z_weights, c))
    greet((section, y, z_rows, c))
    greet((beside, y, z, c))
    greet((following, y, z, c))
    greet((previous, y, z, c))
    greet((section, y, z, core))
    lax.fori_loop(1, experts, greet_row, 0)

    weights = ((w_gate, gate_w), (w_up, up_w), (w_down, down_w))
    kept = [
        pltpu.make_async_copy(src, dst.at[0], local_sem.at[i])
        for i, (src, dst) in enumerate(weights)
    ]
    for copy in kept:
        copy.start()

    for copy in kept:
        copy.wait()
    pl.semaphore_wait(barrier, 2 * experts + 4)

    units = w_down.shape[0] - DETOUR
    pieces = PIECES

    def piece_columns(piece):
        start, count = pieces[piece]
        return pl.ds(start * tile, count * tile)

    def detour(which, step):
        if which == 2:
            stops = (
                down_w.at[0, pl.ds(units, DETOUR)],
                passing_w.at[0],
                passing_w.at[1],
                down_w.at[1, pl.ds(units, DETOUR)],
            )
        else:
            columns = piece_columns(0)
            stops = (
                z_out.at[which, :, columns],
                passing_z.at[0, which],
                passing_z.at[1, which],
                z_in.at[which, :, columns],
            )
        along_z = (section, y, z_rows if which == 2 else z_weights, c)
        return send(
            stops[step],
            stops[step + 1],
            d_send,
            which * 3 + step,
            d_recv,
            which * 3 + step,
            along_z if step == 1 else (beside, y, z, c),
        )

    detour(2, 0).start()
    swaps = (
        (gate_w.at[0], gate_w.at[1]),
        (up_w.at[0], up_w.at[1]),
        (down_w.at[0, pl.ds(0, units)], down_w.at[1, pl.ds(0, units)]),
    )
    swapped = [
        send(src, dst, w_send, i, w_recv, i, (section, y, z_weights, c))
        for i, (src, dst) in enumerate(swaps)
    ]
    for copy in swapped:
        copy.start()

    def normalized(ref, slot):
        wide = ref[...].astype(F32)
        inverse = lax.rsqrt(jnp.mean(wide * wide, axis=-1, keepdims=True) + 1e-06)
        staged[slot * tokens : (slot + 1) * tokens] = (wide * inverse * gain[...]).astype(BF16)
        return inverse

    normalized(fwd_act, 0)
    bwd_inverse = normalized(bwd_act, 1)
    staged[2 * tokens :] = (as_column(bwd_gate[...]) * bwd_grad[...].astype(F32)).astype(BF16)

    fwd_slots = slot_numbers(fwd_route[...])
    bwd_slots = slot_numbers(bwd_route[...])

    detour(2, 0).wait_recv()
    detour(2, 1).start()

    def targets(slots, offset):
        return slots[2] * SLAB + slots[3] + offset

    target = jnp.concatenate(
        [targets(fwd_slots, 0), targets(bwd_slots, CAP), targets(bwd_slots, 2 * CAP)], axis=1
    ).astype(jnp.int32)
    place = selector(iota((experts * SLAB, 3 * tokens), 0) == target)

    def place_half(k, _):
        def place_tile(i, _):
            source = aligned(k * half + i * tile, tile)
            placed = dot(place, staged[:, source]).astype(BF16)
            outgoing[k, :, aligned(i * tile, tile)] = placed
            return 0

        return lax.fori_loop(0, tiles, place_tile, 0)

    lax.fori_loop(0, 2, place_half, 0)

    def slab(index):
        return aligned(index * SLAB, SLAB)

    def dispatch(step, k):
        there = y_at(step, 1)
        return send(
            outgoing.at[k, slab(there)],
            near.at[slab(me)],
            a_send,
            0,
            a_recv,
            me,
            (section, there, z, k),
        )

    def dispatch_row(step, _):
        dispatch(step, 0).start()
        dispatch(step, 1).start()
        return 0

    stay = pltpu.make_async_copy(outgoing.at[c, slab(y)], near.at[slab(me)], local_sem.at[3])
    stay.start()
    dispatch(0, core).start()
    lax.fori_loop(1, experts, dispatch_row, 0)

    def arrival(index):
        return send(
            outgoing.at[0, slab(0)],
            near.at[slab(index)],
            a_send,
            0,
            a_recv,
            index,
            (section, y, z, core),
        )

    def forward(index):
        return send(
            near.at[slab(index)],
            far.at[slab(index)],
            f_send,
            0,
            f_recv,
            0,
            (section, y, z_rows, c),
        )

    def forward_row(step, _):
        there = y_at(step, -1) * 2
        for from_core in range(2):
            arrival(there + from_core).wait_recv()
            forward(there + from_core).start()
        return 0

    stay.wait()
    forward(me).start()
    arrival(y * 2 + core).wait_recv()
    forward(y * 2 + core).start()
    lax.fori_loop(1, experts, forward_row, 0)

    source = iota((3 * block, slabs * SLAB), 1)
    within = source & (SLAB - 1)
    kind = (within >= CAP).astype(jnp.int32) + (within >= 2 * CAP).astype(jnp.int32)
    target = kind * block + (source // SLAB) * CAP + within - kind * CAP
    dense = selector(
        (iota((3 * block, slabs * SLAB), 0) == target) & (within < 3 * CAP)
    )

    def take_apart(slab_rows, first):
        def apart(i, _):
            columns = aligned(i * tile, tile)
            values = dot(dense, slab_rows[:, columns]).astype(BF16)
            for kind in range(3):
                rows[kind, first : first + block, columns] = values[
                    kind * block : (kind + 1) * block
                ]
            return 0

        lax.fori_loop(0, tiles, apart, 0)

    take_apart(near, 0)
    detour(2, 1).wait_recv()
    detour(2, 2).start()

    def part_of(group):
        return pl.ds(group * block, block)

    def first_products(b, group):
        part = part_of(group)

        def of_rows(kind, _):
            for which, weight in ((0, gate_w), (1, up_w)):
                product = dot(rows[kind, part], weight[b])
                pre[b, 2 * kind + which, part] = product
                pre_out[b, 2 * kind + which, part] = product.astype(BF16)
            return 0

        lax.fori_loop(0, 2, of_rows, 0)

    def down_product(b, part):
        product = dot_nt(rows[2, part], down_w[b])
        pre[b, 4, part] = product
        pre_out[b, 4, part] = product.astype(BF16)

    def cross(index):
        b, values, part = (
            (0, pl.ds(0, 5), part_of(0)),
            (1, pl.ds(0, 4), part_of(0)),
            (0, pl.ds(0, 5), part_of(1)),
            (1, pl.ds(0, 4), part_of(1)),
            (1, pl.ds(4, 1), pl.ds(0, 2 * block)),
        )[index]
        return send(
            pre_out.at[b, values, part],
            pre_in.at[b, values, part],
            c_send,
            index,
            c_recv,
            index,
            (section, y, z, core),
        )

    def crossed(b, which, part):
        return pre[b, which, part] + pre_in[b, which, part].astype(F32)

    def activate(b, part):
        gate_pre = crossed(b, 0, part)
        hidden[b, 0, part] = (
            gate_pre * jax.nn.sigmoid(gate_pre) * crossed(b, 1, part)
        ).astype(BF16)

    def derive(b, part):
        gate_pre = crossed(b, 2, part)
        up_pre = crossed(b, 3, part)
        grad = crossed(b, 4, part)
        logistic = jax.nn.sigmoid(gate_pre)
        hidden[b, 1, part] = (
            grad * up_pre * logistic * (1.0 + gate_pre * (1.0 - logistic))
        ).astype(BF16)
        hidden[b, 2, part] = (grad * gate_pre * logistic).astype(BF16)

    def process(group):
        part = part_of(group)
        first_products(0, group)
        down_product(0, part)
        cross(2 * group).start()
        if group == 0:
            swapped[0].wait_recv()
            swapped[1].wait_recv()
        first_products(1, group)
        cross(2 * group + 1).start()
        cross(2 * group).wait_recv()
        activate(0, part)
        derive(0, part)
        cross(2 * group + 1).wait_recv()
        activate(1, part)

    process(0)

    forwarded = send(near, far, f_send, 0, f_recv, 0, (section, y, z_rows, c))
    forwarded.wait_recv()
    take_apart(far, block)
    process(1)

    everything = pl.ds(0, 2 * block)
    swapped[2].wait_recv()
    detour(2, 2).wait_recv()
    down_product(1, everything)
    cross(4).start()

    def give_back(which, piece):
        columns = piece_columns(piece)
        return send(
            z_out.at[which, :, columns],
            z_in.at[which, :, columns],
            z_send.at[which],
            piece,
            z_recv.at[which],
            piece,
            (section, y, z_rows, c),
        )

    def give_back_all(which, one_tile):
        for piece, (start, count) in enumerate(pieces):
            lax.fori_loop(start, start + count, one_tile, 0)
            if piece == 0:
                detour(which, 0).start()
            else:
                give_back(which, piece).start()
            if which == 1 and piece == 0:
                detour(0, 0).wait_recv()
                detour(0, 1).start()

    def split(which, columns, values):
        own[which, :, columns] = values[:block]
        z_out[which, :, columns] = values[block:].astype(BF16)

    def forward_tile(i, _):
        columns = aligned(i * tile, tile)
        split(
            0,
            columns,
            dot(hidden[0, 0], down_w[0, :, columns]) + dot(hidden[1, 0], down_w[1, :, columns]),
        )
        return 0

    give_back_all(0, forward_tile)

    cross(4).wait_recv()
    derive(1, everything)

    def backward_tile(i, _):
        columns = aligned(i * tile, tile)
        values = dot_nt(hidden[0, 1], gate_w[0, columns, :])
        values += dot_nt(hidden[1, 1], gate_w[1, columns, :])
        values += dot_nt(hidden[0, 2], up_w[0, columns, :])
        values += dot_nt(hidden[1, 2], up_w[1, columns, :])
        split(1, columns, values)
        return 0

    give_back_all(1, backward_tile)

    back = iota((slabs * BACK, block), 0)
    place = back & (BACK - 1)
    spread = selector(
        (iota((slabs * BACK, block), 1) == (back // BACK) * CAP + place) & (place < CAP)
    )

    def slots_of(index):
        return aligned(index * BACK, BACK)

    def returning(which, piece, step, to_core):
        there = y_at(step, 1)
        columns = piece_columns(piece)
        return send(
            y_out.at[which, slots_of(there * 2 + to_core), columns],
            y_in.at[which, c, slots_of(y), columns],
            y_send,
            which,
            y_recv.at[which],
            piece,
            (section, there, z, to_core),
        )

    def staying(which, piece):
        columns = piece_columns(piece)
        return pltpu.make_async_copy(
            y_out.at[which, slots_of(me), columns],
            y_in.at[which, c, slots_of(y), columns],
            local_sem.at[4 + which * len(PIECES) + piece],
        )

    def send_back(which, piece):
        if piece == 0:
            detour(which, 2).wait_recv()
        else:
            give_back(which, piece).wait_recv()
        first, count = pieces[piece]

        def spread_tile(i, _):
            columns = aligned(i * tile, tile)
            total = (own[which, :, columns] + z_in[which, :, columns].astype(F32)).astype(BF16)
            y_out[which, :, columns] = dot(spread, total).astype(BF16)
            return 0

        lax.fori_loop(first, first + count, spread_tile, 0)

        def return_row(step, _):
            returning(which, piece, step, 0).start()
            returning(which, piece, step, 1).start()
            return 0

        staying(which, piece).start()
        returning(which, piece, 0, core).start()
        lax.fori_loop(1, experts, return_row, 0)

    others = pl.ds(0, (slabs - 1) * BACK)

    def collect(which, piece):
        staying(which, piece).wait()
        part = y_out.at[which, others, piece_columns(piece)]
        send(
            part, part, y_send, which, y_recv.at[which], piece, (section, y, z, core)
        ).wait_recv()

    detour(1, 0).wait_recv()
    detour(1, 1).start()
    send_back(0, 1)
    detour(0, 1).wait_recv()
    detour(0, 2).start()
    detour(1, 1).wait_recv()
    detour(1, 2).start()
    send_back(0, 2)
    send_back(0, 0)
    send_back(1, 1)
    send_back(1, 0)
    send_back(1, 2)

    def picking(slots):
        target = (slots[0] * BACK + slots[1]).astype(jnp.int32)
        return selector(iota((tokens, experts * BACK), 1) == target)

    pick_fwd = picking(fwd_slots)
    fwd_scale = as_column(fwd_gate[...])
    for piece in (1, 2, 0):
        start, count = pieces[piece]
        collect(0, piece)
        for k in range(2):

            def finish(i, _):
                columns = aligned(k * half + i * tile, tile)
                mixed = dot(pick_fwd, y_in[0, k, :, aligned(i * tile, tile)])
                results[0, :, columns] = (
                    fwd_act[:, columns].astype(F32) + fwd_scale * mixed
                ).astype(BF16)
                return 0

            lax.fori_loop(start, start + count, finish, 0)
    to_next = send(results.at[0], fwd_out, p_send, 0, p_recv, 0, (following, y, z, c))
    to_next.start()

    pick_bwd = picking(bwd_slots)
    dotted = jnp.zeros((tokens, tile), F32)
    for piece in (1, 0, 2):
        start, count = pieces[piece]
        collect(1, piece)
        for k in range(2):

            def gather(i, dotted):
                columns = aligned(k * half + i * tile, tile)
                scaled = gain[:, columns] * dot(pick_bwd, y_in[1, k, :, aligned(i * tile, tile)])
                v_rows[:, columns] = scaled
                return dotted + scaled * bwd_act[:, columns].astype(F32)

            dotted = lax.fori_loop(start, start + count, gather, dotted)
    mean = jnp.sum(dotted, axis=-1, keepdims=True) / width
    factor = bwd_inverse * bwd_inverse * bwd_inverse * mean

    def backward_finish(i, _):
        columns = aligned(i * tile, tile)
        results[1, :, columns] = (
            bwd_grad[:, columns].astype(F32)
            + v_rows[:, columns] * bwd_inverse
            - bwd_act[:, columns].astype(F32) * factor
        ).astype(BF16)
        return 0

    lax.fori_loop(0, 2 * tiles, backward_finish, 0)
    to_previous = send(results.at[1], bwd_out, p_send, 1, p_recv, 1, (previous, y, z, c))
    to_previous.start()

    for copy in swapped:
        copy.wait_send()
    for which in range(3):
        for step in range(3):
            detour(which, step).wait_send()
    for which in range(2):
        part = y_out.at[which, others]
        send(
            part, part, y_send, which, y_recv.at[which], 0, (section, y, z, core)
        ).wait_send()
        for piece in range(1, len(pieces)):
            give_back(which, piece).wait_send()
    part = near.at[pl.ds(0, (slabs - 1) * SLAB)]
    send(part, part, a_send, 0, a_recv, 0, (section, y, z, core)).wait_send()
    forwarded.wait_send()
    for index in range(5):
        cross(index).wait_send()
    to_next.wait()
    to_previous.wait()


def body(
    fwd_act,
    fwd_route,
    fwd_gate,
    bwd_act,
    bwd_grad,
    bwd_route,
    bwd_gate,
    norm_gain,
    w_gate,
    w_up,
    w_down,
):
    experts = lax.axis_size("ep_0")
    _, tokens, width = fwd_act.shape
    _, _, half, units = w_gate.shape
    slabs = 2 * experts
    block = slabs * CAP
    dma = pltpu.SemaphoreType.DMA
    vmem = pl.BlockSpec(memory_space=pltpu.VMEM)
    anywhere = pl.BlockSpec(memory_space=pl.ANY)
    outs = pl.pallas_call(
        functools.partial(kernel, experts),
        out_shape=[jax.ShapeDtypeStruct((tokens, width), BF16)] * 2,
        in_specs=[vmem] * 8 + [anywhere] * 3,
        out_specs=[vmem] * 2,
        scratch_shapes=[
            pltpu.VMEM((3 * tokens, width), BF16),
            pltpu.VMEM((2, experts * SLAB, half), BF16),
            pltpu.VMEM((slabs * SLAB, half), BF16),
            pltpu.VMEM((slabs * SLAB, half), BF16),
            pltpu.VMEM((3, 2 * block, half), BF16),
            pltpu.VMEM((2, half, units), BF16),
            pltpu.VMEM((2, half, units), BF16),
            pltpu.VMEM((2, units, half), BF16),
            pltpu.VMEM((2, 5, 2 * block, units), F32),
            pltpu.VMEM((2, 5, 2 * block, units), BF16),
            pltpu.VMEM((2, 5, 2 * block, units), BF16),
            pltpu.VMEM((2, 3, 2 * block, units), BF16),
            pltpu.VMEM((2, block, half), F32),
            pltpu.VMEM((2, block, half), BF16),
            pltpu.VMEM((2, block, half), BF16),
            pltpu.VMEM((2, slabs * BACK, half), BF16),
            pltpu.VMEM((2, 2, experts * BACK, half), BF16),
            pltpu.VMEM((tokens, width), F32),
            pltpu.VMEM((2, tokens, width), BF16),
            pltpu.VMEM((2, DETOUR, half), BF16),
            pltpu.VMEM((2, 2, block, PIECES[0][1] * 256), BF16),
            dma((4 + 2 * len(PIECES),)),
            dma((3,)),
            dma((3,)),
            dma((1,)),
            dma((slabs,)),
            dma((1,)),
            dma((1,)),
            dma((5,)),
            dma((5,)),
            dma((2, len(PIECES))),
            dma((2, len(PIECES))),
            dma((2,)),
            dma((2, len(PIECES))),
            dma((2,)),
            dma((2,)),
            dma((9,)),
            dma((9,)),
        ],
        compiler_params=pltpu.CompilerParams(
            collective_id=0, has_side_effects=True, vmem_limit_bytes=60 * 1024 * 1024
        ),
        name="relay_layer",
    )(
        fwd_act[0],
        fwd_route[:, :, 0],
        fwd_gate[:, :, 0],
        bwd_act[0],
        bwd_grad[0],
        bwd_route[:, :, 0],
        bwd_gate[:, :, 0],
        norm_gain,
        w_gate[0, 0],
        w_up[0, 0],
        w_down[0, 0],
    )
    return tuple(out[None] for out in outs)


def solution(mesh):
    sections = mesh.shape["pp"]
    split = Mesh(
        mesh.devices.reshape(sections, mesh.shape["ep"] // 8, 4, 2), ("pp", "ep_0", "ep_1", "ep_2")
    )
    rows = P("pp", EP, None)
    weights = P("pp", EP, None, None)
    return jax.shard_map(
        body,
        mesh=split,
        in_specs=(rows,) * 7 + (P("pp", None),) + (weights,) * 3,
        out_specs=(rows, rows),
        check_vma=False,
    )
```
